768 devices in a mesh: ctx: 384 (over x, z, y_lo, core), grp: 2 (over y_hi).
Axes of the slice: x: 4, y: 8 (y_hi: 2, y_lo: 4; y = y_hi * 4 + y_lo), z: 12, core: 2. Of those that a mesh axis runs over, the one named last changes fastest.
Arguments:
- doc_lengths: int32 [192], replicated, may hold values from 1 to 8192, 98304 in all
- query_raw: bfloat16 [98304, 2048], P(('ctx', 'grp')), may hold values from -40 to 40
- key_raw: bfloat16 [98304, 1024], P(('ctx', 'grp')), may hold values from -40 to 40
- value_matrix: bfloat16 [98304, 1024], P(('ctx', 'grp')), may hold values from -5 to 5
- out_grad: bfloat16 [98304, 2048], P(('ctx', 'grp')), may hold values from -5 to 5
- query_gain: float32 [128], replicated, may hold values from 0.5 to 6
- key_gain: float32 [128], replicated, may hold values from 0.5 to 6
Outputs:
- grad_query: bfloat16 [98304, 2048], P(('ctx', 'grp'))
- grad_key: bfloat16 [98304, 1024], P(('ctx', 'grp'))
- grad_value: bfloat16 [98304, 1024], P(('ctx', 'grp'))
- grad_query_gain: float32 [128], replicated
- grad_key_gain: float32 [128], replicated
The draws below stay inside these ranges and needn't reach their ends.
Inputs may be any that keep to these rules, and one draw needn't show every extreme that they name: `doc_lengths`: lengths of the packed documents in order; they sum to 98304, and one of them is exactly 8192.
All inputs are finite; a program needn't handle non-finite values.
Results may differ from the reference program's by a relative error of at most 0.035.
The reference program's roundings to bfloat16 on the way (of `probs_low` and `score_grad`) count: a program that leaves them out, or rounds other values in their place, can miss the bound.
Values may be sent and summed in bfloat16 or wider, within the bound.
A program may use at most 64 MiB of HBM per device.

```python
import math
import jax
import jax.numpy as jnp
import numpy as np
from jax import lax

QUERY_HEADS = 16
KEY_VALUE_HEADS = 8
HEAD_SIZE = 128
WINDOW = 256
TOK_DEV = 128
PACKED_TOKENS = 98304
DOCS = 192
MOST = 8192


def row_scales(key, row_count):
    return jnp.exp(jax.random.uniform(key, (row_count, 1), jnp.float32, 0.0, math.log(10.0)))


def draw_query_raw(key, part):
    scale_factors = row_scales(jax.random.fold_in(key, 1), PACKED_TOKENS)
    starting_rows = jnp.clip(jax.random.normal(jax.random.fold_in(key, 2), (PACKED_TOKENS, QUERY_HEADS, HEAD_SIZE), jnp.float32), -4.0, 4.0)
    return (starting_rows.reshape(PACKED_TOKENS, QUERY_HEADS * HEAD_SIZE) * scale_factors).astype(jnp.bfloat16)


def draw_key_raw(key, part):
    scale_factors = row_scales(jax.random.fold_in(key, 3), PACKED_TOKENS)
    starting_rows = jnp.clip(jax.random.normal(jax.random.fold_in(key, 4), (PACKED_TOKENS, KEY_VALUE_HEADS, HEAD_SIZE), jnp.float32), -4.0, 4.0)
    return (starting_rows.reshape(PACKED_TOKENS, KEY_VALUE_HEADS * HEAD_SIZE) * scale_factors).astype(jnp.bfloat16)


def draw_query_gain(key, part):
    return jnp.exp(jax.random.uniform(jax.random.fold_in(key, 21), (HEAD_SIZE,), jnp.float32, math.log(0.5), math.log(2.0)))


def draw_key_gain(key, part):
    return jnp.exp(jax.random.uniform(jax.random.fold_in(key, 22), (HEAD_SIZE,), jnp.float32, math.log(0.5), math.log(2.0)))


def shard_levels(key, dims, shards, smallest, high):
    loudness = 1.0
    for position, parts in shards:
        draws = jax.random.uniform(jax.random.fold_in(jax.random.fold_in(key, 6), position), (parts,), jnp.float32, smallest / len(shards), high / len(shards))
        loudness = loudness * jnp.repeat(jnp.exp(draws), dims[position] // parts).reshape((-1,) + (1,) * (len(dims) - 1 - position))
    return loudness


def profile(amount, total, most, slope):
    loads = [(1 << 20) // math.isqrt(rank ** slope) + 1 for rank in range(2, amount + 1)]
    surplus, holding = total - most - (amount - 1), [1] * (amount - 1)
    while surplus > 0:
        candidates = [i for i in range(amount - 1) if holding[i] < most]
        mass, remaining = sum([loads[i] for i in candidates]), surplus
        for i in candidates:
            more = min(most - holding[i], max(1, remaining * loads[i] // mass), surplus)
            holding[i] = holding[i] + more
            surplus = surplus - more
    return np.array([most] + holding)


def uneven_parts(rng, number_of, total, most, lean):
    if number_of == 2:
        one = jax.random.randint(rng, (), max(1, total - most), min(most, total - 1) + 1)
        return jnp.stack([one, total - one])
    sizes = jnp.asarray(profile(number_of, total, most, lean), jnp.int32)
    pairs = (number_of - 1) // 2
    giver, receiver = sizes[1:1 + 2 * pairs:2], sizes[2:2 + 2 * pairs:2]
    room = jnp.minimum(giver - 1, most - receiver)
    shifted = jax.random.randint(jax.random.fold_in(rng, 1), (pairs,), 0, 1 << 20) % (room + 1)
    sizes = sizes.at[1:1 + 2 * pairs:2].set(giver - shifted).at[2:2 + 2 * pairs:2].set(receiver + shifted)
    return sizes[jax.random.permutation(jax.random.fold_in(rng, 2), number_of)]


def noise(stream_key, dims, deviation, bound, shards=(), held_as=jnp.bfloat16):
    level = shard_levels(stream_key, dims, shards, -0.22, 0.18) if shards else 1.0
    values = jax.random.normal(stream_key, dims, jnp.float32) * deviation * level
    return jnp.minimum(jnp.maximum(values, -bound), bound).astype(held_as)


def setup_inputs(seed: int = 0) -> dict:
    splits = jax.random.split(jax.random.key(seed), 8)
    doc_lengths = uneven_parts(splits[0], DOCS, PACKED_TOKENS, MOST, 2).astype(jnp.int32)
    query_raw = draw_query_raw(jax.random.fold_in(splits[7], 71), 0)
    key_raw = draw_key_raw(jax.random.fold_in(splits[7], 71), 0)
    value_matrix = noise(splits[3], (PACKED_TOKENS, KEY_VALUE_HEADS * HEAD_SIZE), 1.0, 5.0, ((0, 768),))
    out_grad = noise(splits[4], (PACKED_TOKENS, QUERY_HEADS * HEAD_SIZE), 1.0, 5.0, ((0, 768),))
    query_gain = draw_query_gain(jax.random.fold_in(splits[7], 71), 0)
    key_gain = draw_key_gain(jax.random.fold_in(splits[7], 71), 0)
    return {"doc_lengths": doc_lengths, "query_raw": query_raw, "key_raw": key_raw, "value_matrix": value_matrix, "out_grad": out_grad, "query_gain": query_gain, "key_gain": key_gain}


eps_norm = 1e-06
score_scale = 168.0 ** (-0.5)
rope_base = 10000.0
masked_score = -1e+30

def doc_places(token_ids, doc_lengths):
    doc_ends = jnp.cumsum(doc_lengths).astype(jnp.int32)
    before = doc_ends[None, :] <= token_ids[:, None]
    doc_ids = lax.optimization_barrier(jnp.sum(before.astype(jnp.int32), axis=1)).astype(jnp.int32)
    starts = lax.optimization_barrier(jnp.max(jnp.where(before, doc_ends[None, :], 0), axis=1)).astype(jnp.int32)
    return (doc_ids, (token_ids - starts).astype(jnp.int32))

def rotary_tables(positions):
    half_width = HEAD_SIZE // 2
    frequency = rope_base ** (-2.0 * jnp.arange(half_width, dtype=jnp.float32) / HEAD_SIZE)
    angles = positions.astype(jnp.float32)[:, None] * frequency[None, :]
    return (jnp.cos(angles), jnp.sin(angles))

def norm_rotate(raw_rows, norm_gain, cosine, sine_table):
    row_count = raw_rows.shape[0]
    raw_values = raw_rows.astype(jnp.float32).reshape(row_count, -1, HEAD_SIZE)
    row_scale = lax.rsqrt(lax.optimization_barrier(jnp.mean(raw_values * raw_values, axis=-1, keepdims=True)) + eps_norm)
    normed = raw_values * row_scale * norm_gain
    front_half = normed[..., :HEAD_SIZE // 2]
    back_half = normed[..., HEAD_SIZE // 2:]
    cos_rows = cosine[:, None, :]
    sin_rows = sine_table[:, None, :]
    rotated = jnp.concatenate([front_half * cos_rows - back_half * sin_rows, back_half * cos_rows + front_half * sin_rows], -1)
    return rotated.reshape(row_count, -1).astype(jnp.bfloat16)

def unrotate_norm(grad_rot, raw_rows, norm_gain, cosine, sine_table):
    row_count = grad_rot.shape[0]
    grad_rows = grad_rot.reshape(row_count, -1, HEAD_SIZE)
    front_half = grad_rows[..., :HEAD_SIZE // 2]
    back_half = grad_rows[..., HEAD_SIZE // 2:]
    cos_rows = cosine[:, None, :]
    sin_rows = sine_table[:, None, :]
    grad_normed = jnp.concatenate([front_half * cos_rows + back_half * sin_rows, back_half * cos_rows - front_half * sin_rows], -1)
    raw_values = raw_rows.astype(jnp.float32).reshape(row_count, -1, HEAD_SIZE)
    row_scale = lax.rsqrt(lax.optimization_barrier(jnp.mean(raw_values * raw_values, axis=-1, keepdims=True)) + eps_norm)
    gain_grad = lax.optimization_barrier(jnp.sum(grad_normed * raw_values * row_scale, axis=(0, 1)))
    weighted = grad_normed * norm_gain
    raw_grad = row_scale * weighted - raw_values * row_scale ** 3 * lax.optimization_barrier(jnp.mean(weighted * raw_values, axis=-1, keepdims=True))
    return (raw_grad.reshape(row_count, -1).astype(jnp.bfloat16), gain_grad)

def visibility(own_tokens, own_docs, key_tokens, key_docs):
    same_doc = own_docs[:, None] == key_docs[None, :]
    causal = key_tokens[None, :] <= own_tokens[:, None]
    inside = own_tokens[:, None] - key_tokens[None, :] < WINDOW
    real_key = key_tokens[None, :] >= 0
    return same_doc & causal & inside & real_key

def head_grads(queries, grads_out, key_block, value_block, visible):
    queries = queries.astype(jnp.float32)
    grads_out = grads_out.astype(jnp.float32)
    key_block = key_block.astype(jnp.float32)
    value_block = value_block.astype(jnp.float32)
    scores = jnp.einsum('qhd,kd->hqk', queries, key_block) * score_scale
    scores = jnp.where(visible[None], scores, masked_score)
    row_top = lax.optimization_barrier(jnp.max(scores, axis=-1, keepdims=True))
    exps_rows = jnp.exp(scores - row_top)
    weights = exps_rows / lax.optimization_barrier(jnp.sum(exps_rows, axis=-1, keepdims=True))
    probs_low = weights.astype(jnp.bfloat16).astype(jnp.float32)
    prob_grad = jnp.einsum('qhd,kd->hqk', grads_out, value_block)
    row_delta = lax.optimization_barrier(jnp.sum(weights * prob_grad, axis=-1, keepdims=True))
    score_grad = (weights * (prob_grad - row_delta)).astype(jnp.bfloat16).astype(jnp.float32)
    query_grad = jnp.einsum('hqk,kd->qhd', score_grad, key_block) * score_scale
    key_grad = jnp.einsum('hqk,qhd->kd', score_grad, queries) * score_scale
    value_grad = jnp.einsum('hqk,qhd->kd', probs_low, grads_out)
    return (query_grad, key_grad, value_grad)

def round_far(term_rows, cut_rows):
    low_rows = lax.optimization_barrier(term_rows[:cut_rows].astype(jnp.bfloat16))
    return jnp.concatenate([low_rows.astype(jnp.float32), term_rows[cut_rows:]], 0)

def reference(doc_lengths, query_raw, key_raw, value_matrix, out_grad, query_gain, key_gain):
    halo_depth = WINDOW // TOK_DEV
    key_count = (halo_depth + 1) * TOK_DEV
    blocks = PACKED_TOKENS // TOK_DEV
    group_width = QUERY_HEADS // KEY_VALUE_HEADS
    padding_rows = halo_depth * TOK_DEV
    all_tokens = jnp.arange(PACKED_TOKENS, dtype=jnp.int32)
    all_docs, all_pos = doc_places(all_tokens, doc_lengths)
    cosine, sine_table = rotary_tables(all_pos)
    query_rot = norm_rotate(query_raw, query_gain, cosine, sine_table)
    rotated_keys = norm_rotate(key_raw, key_gain, cosine, sine_table)
    padded_keys = jnp.concatenate([jnp.zeros((padding_rows, KEY_VALUE_HEADS * HEAD_SIZE), jnp.bfloat16), rotated_keys], 0)
    padded_values = jnp.concatenate([jnp.zeros((padding_rows, KEY_VALUE_HEADS * HEAD_SIZE), jnp.bfloat16), value_matrix], 0)

    def block_step(carried, block_index):
        key_acc, value_acc, gain_acc = carried
        row_start = (block_index * TOK_DEV).astype(jnp.int32)
        queries = lax.dynamic_slice_in_dim(query_rot, row_start, TOK_DEV, 0)
        grads_out = lax.dynamic_slice_in_dim(out_grad, row_start, TOK_DEV, 0)
        raw_block = lax.dynamic_slice_in_dim(query_raw, row_start, TOK_DEV, 0)
        cos_block = lax.dynamic_slice_in_dim(cosine, row_start, TOK_DEV, 0)
        sin_block = lax.dynamic_slice_in_dim(sine_table, row_start, TOK_DEV, 0)
        key_block = lax.dynamic_slice_in_dim(padded_keys, row_start, key_count, 0)
        value_block = lax.dynamic_slice_in_dim(padded_values, row_start, key_count, 0)
        key_tokens = (row_start - padding_rows + jnp.arange(key_count, dtype=jnp.int32)).astype(jnp.int32)
        key_docs, unused_pos = doc_places(key_tokens, doc_lengths)
        own_tokens = key_tokens[padding_rows:]
        own_docs = key_docs[padding_rows:]
        visible = visibility(own_tokens, own_docs, key_tokens, key_docs)
        query_parts, key_parts, value_parts = ([], [], [])
        for key_value_head in range(KEY_VALUE_HEADS):
            key_cols = slice(key_value_head * HEAD_SIZE, (key_value_head + 1) * HEAD_SIZE)
            query_cols = slice(key_value_head * group_width * HEAD_SIZE, (key_value_head + 1) * group_width * HEAD_SIZE)
            query_grad, key_grad, value_grad = head_grads(queries[:, query_cols].reshape(TOK_DEV, group_width, HEAD_SIZE), grads_out[:, query_cols].reshape(TOK_DEV, group_width, HEAD_SIZE), key_block[:, key_cols], value_block[:, key_cols], visible)
            query_parts.append(query_grad.reshape(TOK_DEV, group_width * HEAD_SIZE))
            key_parts.append(key_grad)
            value_parts.append(value_grad)
        query_term = jnp.concatenate(query_parts, 1)
        key_term = round_far(jnp.concatenate(key_parts, 1), padding_rows)
        value_term = round_far(jnp.concatenate(value_parts, 1), padding_rows)
        key_acc = lax.dynamic_update_slice_in_dim(key_acc, lax.dynamic_slice_in_dim(key_acc, row_start, key_count, 0) + key_term, row_start, 0)
        value_acc = lax.dynamic_update_slice_in_dim(value_acc, lax.dynamic_slice_in_dim(value_acc, row_start, key_count, 0) + value_term, row_start, 0)
        raw_grad, gain_part = unrotate_norm(query_term, raw_block, query_gain, cos_block, sin_block)
        return ((key_acc, value_acc, gain_acc + gain_part), raw_grad)
    initial_state = (jnp.zeros((PACKED_TOKENS + padding_rows, KEY_VALUE_HEADS * HEAD_SIZE), jnp.float32), jnp.zeros((PACKED_TOKENS + padding_rows, KEY_VALUE_HEADS * HEAD_SIZE), jnp.float32), jnp.zeros((HEAD_SIZE,), jnp.float32))
    final_state, query_blocks = lax.scan(block_step, initial_state, jnp.arange(blocks, dtype=jnp.int32))
    key_acc, value_acc, grad_query_gain = final_state
    grad_query = query_blocks.reshape(PACKED_TOKENS, QUERY_HEADS * HEAD_SIZE)
    grad_key, grad_key_gain = unrotate_norm(key_acc[padding_rows:], key_raw, key_gain, cosine, sine_table)
    grad_value = value_acc[padding_rows:].astype(jnp.bfloat16)
    return (grad_query, grad_key, grad_value, grad_query_gain, grad_key_gain)
```

```python
import functools

import jax
import jax.numpy as jnp
import numpy as np
from jax import lax
from jax.experimental import pallas as pl
from jax.experimental.pallas import tpu as pltpu
from jax.sharding import PartitionSpec as P

HEAD = 128
HALF = HEAD // 2
WINDOW = 256
TOK = 128
KEYS = WINDOW + TOK
EPS = 1e-06
SCALE = 168.0 ** (-0.5)
BASE = 10000.0
MASKED = -1e30
RING = 16
ZS = 12
XS = 4
MESH = pl.DeviceIdType.MESH
F32 = jnp.float32
BF16 = jnp.bfloat16
NT = (((1,), (1,)), ((), ()))
NN = (((1,), (0,)), ((), ()))
TN = (((0,), (0,)), ((), ()))


def place(block):
    return {"ctx": block // 2, "grp": block % 2}


def mm(a, b, dims):
    return lax.dot_general(a, b, dims, preferred_element_type=F32)


def kernel(devices, docs, heads, group, lens_ref, freq_ref, qgain_ref, kgain_ref, q_hbm, k_hbm, v_hbm, g_hbm,
           dq_ref, dk_ref, dv_ref, gains_ref,
           q, go, kv, dkv, term, back, cosd, sins, bias, box, zbox, total,
           load_sem, fs_sem, fr_sem, bs_sem, br_sem, as_sem, ar_sem):
    me = lax.axis_index("ctx") * 2 + lax.axis_index("grp")
    slot_in_ring = me % RING
    ring = me // RING
    z = ring % ZS
    x = ring // ZS
    quad = z % 4
    zgroup = z // 4

    barrier = pltpu.get_barrier_semaphore()

    def greet(block):
        pl.semaphore_signal(barrier, inc=1, device_id=place(block), device_id_type=MESH)

    for hop in (1, 2):
        @pl.when(me >= hop)
        def _():
            greet(me - hop)

        @pl.when(me + hop < devices)
        def _():
            greet(me + hop)

    def ring_peer(i):
        return ring * RING + (slot_in_ring + i) % RING

    def quad_peer(i):
        return (x * ZS + zgroup * 4 + (quad + i) % 4) * RING + slot_in_ring

    def x_peer(i):
        return (((x + i) % XS) * ZS + z) * RING + slot_in_ring

    def group_peer(other):
        return (x * ZS + other * 4 + quad) * RING + slot_in_ring

    @pl.loop(1, RING)
    def _(i):
        greet(ring_peer(i))

    for i in range(1, 4):
        greet(quad_peer(i))
        greet(x_peer(i))

    @pl.when(zgroup == 1)
    def _():
        greet(group_peer(0))
        greet(group_peer(2))

    @pl.when(zgroup != 1)
    def _():
        greet(group_peer(1))

    loads = [
        pltpu.make_async_copy(k_hbm, kv.at[0, 2], load_sem.at[0]),
        pltpu.make_async_copy(v_hbm, kv.at[1, 2], load_sem.at[1]),
        pltpu.make_async_copy(q_hbm, q, load_sem.at[2]),
        pltpu.make_async_copy(g_hbm, go, load_sem.at[3]),
    ]
    for load in loads:
        load.start()

    near = (jnp.minimum(me, 1) + jnp.minimum(me // 2, 1)
            + jnp.minimum(devices - 1 - me, 1) + jnp.minimum((devices - 1 - me) // 2, 1))
    pl.semaphore_wait(barrier, near + (RING - 1) + 3 + 3 + 1 + (zgroup % 2))

    def columns(head):
        return pl.ds(pl.multiple_of(head * HEAD, HEAD), HEAD)

    def forward(hop, which, head):
        source = (k_hbm, v_hbm)[which]
        return pltpu.make_async_remote_copy(
            src_ref=source.at[:, columns(head)],
            dst_ref=kv.at[which, 2 - hop, :, columns(head)],
            send_sem=fs_sem.at[hop - 1, which, head],
            recv_sem=fr_sem.at[hop - 1, which, head],
            device_id=place(lax.rem(me + hop, devices)),
            device_id_type=MESH,
        )

    def backward(hop, which, head):
        return pltpu.make_async_remote_copy(
            src_ref=term.at[which, 2 - hop, :, columns(head)],
            dst_ref=back.at[which, hop - 1, :, columns(head)],
            send_sem=bs_sem.at[hop - 1, which, head],
            recv_sem=br_sem.at[hop - 1, which, head],
            device_id=place(lax.rem(me - hop + devices, devices)),
            device_id_type=MESH,
        )

    @pl.loop(0, heads)
    def _(head):
        for hop in (1, 2):
            @pl.when(me + hop < devices)
            def _():
                for which in (0, 1):
                    forward(hop, which, head).start()

    for hop in (1, 2):
        @pl.when(me < hop)
        def _():
            kv[:, 2 - hop] = jnp.zeros((2, TOK, heads * HEAD), BF16)

        @pl.when(me + hop >= devices)
        def _():
            back[:, hop - 1] = jnp.zeros((2, TOK, heads * HEAD), BF16)

    wide = lens_ref.shape[1]
    lens = lens_ref[...]
    down = lax.broadcasted_iota(jnp.int32, (wide, wide), 0)
    along = lax.broadcasted_iota(jnp.int32, (wide, wide), 1)
    real_down = lax.broadcasted_iota(jnp.int32, (wide, 1), 0) < docs
    real_along = lax.broadcasted_iota(jnp.int32, (1, wide), 1) < docs
    lens_all = jnp.broadcast_to(lens, (wide, wide))
    lens_col = jnp.sum(jnp.where(down == along, lens_all, 0.0), axis=1, keepdims=True)
    ends_row = jnp.sum(jnp.where(down <= along, lens_col, 0.0), axis=0, keepdims=True)
    ends_col = jnp.sum(jnp.where(along <= down, lens_all, 0.0), axis=1, keepdims=True)
    ends_row = jnp.where(real_along, ends_row, 1e9)
    ends_col = jnp.where(real_down, ends_col, 1e9)
    first = (me - 2) * TOK
    key_tok = (first + lax.broadcasted_iota(jnp.int32, (KEYS, 1), 0)).astype(F32)
    own_tok = (first + WINDOW + lax.broadcasted_iota(jnp.int32, (1, TOK), 1)).astype(F32)
    key_before = ends_row <= key_tok
    key_start = jnp.max(jnp.where(key_before, ends_row, 0.0), axis=1, keepdims=True)
    key_doc = jnp.sum(jnp.where(key_before, 1.0, 0.0), axis=1, keepdims=True)
    own_doc = jnp.sum(jnp.where(ends_col <= own_tok, 1.0, 0.0), axis=0, keepdims=True)
    apart = own_tok - key_tok
    visible = (key_doc == own_doc) & (apart >= 0.0) & (apart < float(WINDOW)) & (key_tok >= 0.0)
    bias[...] = jnp.where(visible, 0.0, MASKED)
    angle = (key_tok - key_start) * freq_ref[...]
    cosd[...] = jnp.cos(angle)
    front = lax.broadcasted_iota(jnp.int32, (1, HEAD), 1) < HALF
    sine = jnp.sin(angle)
    sins[...] = jnp.where(front, -sine, sine)

    for load in loads:
        load.wait()

    kgain = kgain_ref[...]
    qgain = qgain_ref[...]
    own = pl.ds(WINDOW, TOK)

    def scale_of(values):
        return lax.rsqrt(jnp.mean(values * values, axis=-1, keepdims=True) + EPS)

    def rotate(normed, cosine, sine):
        return normed * cosine + pltpu.roll(normed, HALF, 1) * sine

    def unrotate(grads, cosine, sine):
        return grads * cosine - pltpu.roll(grads, HALF, 1) * sine

    def raw_grad(grad_normed, values, scale, gain):
        weighted = grad_normed * gain
        return (scale * weighted
                - values * (scale * scale * scale) * jnp.mean(weighted * values, axis=-1, keepdims=True))

    def head_step(head, sums):
        q_sum, k_sum = sums
        for hop in (1, 2):
            @pl.when(me >= hop)
            def _():
                for which in (0, 1):
                    forward(hop, which, head).wait_recv()

        cols = columns(head)
        keys = kv[0, :, :, cols].reshape(KEYS, HEAD).astype(F32)
        values = kv[1, :, :, cols].reshape(KEYS, HEAD)
        k_scale = scale_of(keys)
        k_unit = keys * k_scale
        k_rot = rotate(k_unit * kgain, cosd[...], sins[...]).astype(BF16)
        q_cols = [columns(head * group + i) for i in range(group)]
        q_rot = []
        for c in q_cols:
            raw = q[:, c].astype(F32)
            q_rot.append(rotate(raw * scale_of(raw) * qgain, cosd[own, :], sins[own, :]).astype(BF16))
        q_rot = jnp.concatenate(q_rot, 0)
        g_out = jnp.concatenate([go[:, c] for c in q_cols], 0)
        masks = jnp.concatenate([bias[...]] * group, 1)
        scores = mm(k_rot, q_rot, NT) * SCALE + masks
        top = jnp.max(scores, axis=0, keepdims=True)
        exps = jnp.exp(scores - top)
        probs = exps * (1.0 / jnp.sum(exps, axis=0, keepdims=True))
        prob_grad = mm(values, g_out, NT)
        delta = jnp.sum(probs * prob_grad, axis=0, keepdims=True)
        score_grad = (probs * (prob_grad - delta)).astype(BF16)
        v_term = mm(probs.astype(BF16), g_out, NN)
        k_term = mm(score_grad, q_rot, NN) * SCALE
        v_far = v_term[:WINDOW].astype(BF16)
        k_far = k_term[:WINDOW].astype(BF16)
        term[0, :, :, cols] = k_far.reshape(2, TOK, HEAD)
        term[1, :, :, cols] = v_far.reshape(2, TOK, HEAD)
        for hop in (1, 2):
            @pl.when(me >= hop)
            def _():
                for which in (0, 1):
                    backward(hop, which, head).start()
        dkv[0, :, cols] = k_term[WINDOW:]
        dkv[1, :, cols] = v_term[WINDOW:]
        q_term = mm(score_grad, k_rot, TN) * SCALE
        k_all = jnp.concatenate([k_far.astype(F32), k_term[WINDOW:]], 0)
        k_sum = k_sum + jnp.sum(unrotate(k_all, cosd[...], sins[...]) * k_unit, axis=0, keepdims=True)
        for i, c in enumerate(q_cols):
            raw = q[:, c].astype(F32)
            scale = scale_of(raw)
            normed = unrotate(q_term[i * TOK:(i + 1) * TOK], cosd[own, :], sins[own, :])
            q_sum = q_sum + jnp.sum(normed * raw * scale, axis=0, keepdims=True)
            dq_ref[:, c] = raw_grad(normed, raw, scale, qgain).astype(BF16)
        return q_sum, k_sum

    zero = jnp.zeros((1, HEAD), F32)
    q_sum, k_sum = lax.fori_loop(0, heads, head_step, (zero, zero))

    row = lax.broadcasted_iota(jnp.int32, (8, HEAD), 0)
    part = jnp.where(row == 0, q_sum, jnp.where(row == 1, k_sum, 0.0))

    def message(source, target, index, peer, sem):
        return pltpu.make_async_remote_copy(
            src_ref=source, dst_ref=target, send_sem=as_sem.at[index], recv_sem=ar_sem.at[sem],
            device_id=place(peer), device_id_type=MESH,
        )

    def summed(values):
        out = values[0]
        for value in values[1:]:
            out = out + value
        return out

    def exchange(part, base, count, mine, peer):
        box[base + mine] = part

        @pl.loop(1, count)
        def _(i):
            message(box.at[base + mine], box.at[base + mine], base + i, peer(i), base + mine).start()

        @pl.loop(1, count)
        def _(i):
            there = base + (mine + i) % count
            message(box.at[there], box.at[there], base + i, peer(i), there).wait_recv()

        @pl.loop(1, count)
        def _(i):
            message(box.at[base + mine], box.at[base + mine], base + i, peer(i), base + mine).wait_send()

        return summed([box[base + i] for i in range(count)])

    part = exchange(part, 0, RING, slot_in_ring, ring_peer)
    part = exchange(part, RING, XS, x, x_peer)
    part = exchange(part, RING + XS, 4, quad, quad_peer)
    last = RING + XS + 4
    zbox[zgroup] = part

    def up(g):
        return message(zbox.at[g], zbox.at[g], last + g, group_peer(1), last + g)

    def answer(g):
        return message(total, total, last + g, group_peer(g), last + 1)

    @pl.when(zgroup == 1)
    def _():
        up(0).wait_recv()
        up(2).wait_recv()
        total[...] = zbox[0] + zbox[1] + zbox[2]
        answer(0).start()
        answer(2).start()

    @pl.when(zgroup != 1)
    def _():
        up(zgroup).start()

    @pl.loop(0, heads)
    def _(head):
        for hop in (1, 2):
            @pl.when(me + hop < devices)
            def _():
                for which in (0, 1):
                    backward(hop, which, head).wait_recv()

        cols = columns(head)
        k_grad = dkv[0, :, cols] + back[0, 0, :, cols].astype(F32) + back[0, 1, :, cols].astype(F32)
        v_grad = dkv[1, :, cols] + back[1, 0, :, cols].astype(F32) + back[1, 1, :, cols].astype(F32)
        dv_ref[:, cols] = v_grad.astype(BF16)
        keys = kv[0, 2, :, cols].astype(F32)
        normed = unrotate(k_grad, cosd[own, :], sins[own, :])
        dk_ref[:, cols] = raw_grad(normed, keys, scale_of(keys), kgain).astype(BF16)

    @pl.when(zgroup == 1)
    def _():
        answer(0).wait_send()
        answer(2).wait_send()

    @pl.when(zgroup != 1)
    def _():
        up(zgroup).wait_send()
        answer(1).wait_recv()

    gains_ref[...] = total[...]

    @pl.loop(0, heads)
    def _(head):
        for hop in (1, 2):
            @pl.when(me + hop < devices)
            def _():
                for which in (0, 1):
                    forward(hop, which, head).wait_send()

            @pl.when(me >= hop)
            def _():
                for which in (0, 1):
                    backward(hop, which, head).wait_send()


def on_device(devices, doc_lengths, query_raw, key_raw, value_matrix, out_grad, query_gain, key_gain):
    heads = key_raw.shape[1] // HEAD
    group = query_raw.shape[1] // key_raw.shape[1]
    docs = doc_lengths.shape[0]
    wide = -(-docs // 128) * 128
    lens = jnp.pad(doc_lengths.astype(F32), (0, wide - docs)).reshape(1, wide)
    lane = np.arange(HEAD) % HALF
    freq = jnp.asarray((np.float64(BASE) ** (-2.0 * lane / HEAD)).astype(np.float32).reshape(1, HEAD))
    vmem = pl.BlockSpec(memory_space=pltpu.VMEM)
    anywhere = pl.BlockSpec(memory_space=pl.ANY)
    width = heads * HEAD
    grad_query, grad_key, grad_value, gains = pl.pallas_call(
        functools.partial(kernel, devices, docs, heads, group),
        out_shape=(
            jax.ShapeDtypeStruct(query_raw.shape, BF16),
            jax.ShapeDtypeStruct(key_raw.shape, BF16),
            jax.ShapeDtypeStruct(key_raw.shape, BF16),
            jax.ShapeDtypeStruct((8, HEAD), F32),
        ),
        in_specs=[vmem] * 4 + [anywhere] * 4,
        out_specs=(vmem, vmem, vmem, vmem),
        scratch_shapes=[
            pltpu.VMEM((TOK, width * group), BF16),
            pltpu.VMEM((TOK, width * group), BF16),
            pltpu.VMEM((2, 3, TOK, width), BF16),
            pltpu.VMEM((2, TOK, width), F32),
            pltpu.VMEM((2, 2, TOK, width), BF16),
            pltpu.VMEM((2, 2, TOK, width), BF16),
            pltpu.VMEM((KEYS, HEAD), F32),
            pltpu.VMEM((KEYS, HEAD), F32),
            pltpu.VMEM((KEYS, HEAD), F32),
            pltpu.VMEM((RING + XS + 4, 8, HEAD), F32),
            pltpu.VMEM((3, 8, HEAD), F32),
            pltpu.VMEM((8, HEAD), F32),
            pltpu.SemaphoreType.DMA((4,)),
            pltpu.SemaphoreType.DMA((2, 2, heads)),
            pltpu.SemaphoreType.DMA((2, 2, heads)),
            pltpu.SemaphoreType.DMA((2, 2, heads)),
            pltpu.SemaphoreType.DMA((2, 2, heads)),
            pltpu.SemaphoreType.DMA((RING + XS + 4 + 3,)),
            pltpu.SemaphoreType.DMA((RING + XS + 4 + 3,)),
        ],
        compiler_params=pltpu.CompilerParams(
            collective_id=0, has_side_effects=True, vmem_limit_bytes=56 << 20
        ),
    )(lens, freq, query_gain.reshape(1, HEAD), key_gain.reshape(1, HEAD), query_raw, key_raw, value_matrix, out_grad)
    return grad_query, grad_key, grad_value, gains[0], gains[1]


def solution(mesh):
    devices = mesh.devices.size
    rows = P(("ctx", "grp"), None)
    return jax.shard_map(
        functools.partial(on_device, devices),
        mesh=mesh,
        in_specs=(P(), rows, rows, rows, rows, P(), P()),
        out_specs=(rows, rows, rows, P(), P()),
        check_vma=False,
    )
```

```python
import functools

import jax
import jax.numpy as jnp
import numpy as np
from jax import lax
from jax.experimental import pallas as pl
from jax.experimental.pallas import tpu as pltpu
from jax.sharding import PartitionSpec as P

HEAD = 128
HALF = HEAD // 2
WINDOW = 256
TOK = 128
KEYS = WINDOW + TOK
EPS = 1e-06
SCALE = 168.0 ** (-0.5)
BASE = 10000.0
MASKED = -1e30
LOG2E = 1.4426950408889634
AHEAD = 2
HOLD = 4
RING = 16
ZS = 12
XS = 4
MESH = pl.DeviceIdType.MESH
F32 = jnp.float32
BF16 = jnp.bfloat16
NT = (((1,), (1,)), ((), ()))
NN = (((1,), (0,)), ((), ()))
TN = (((0,), (0,)), ((), ()))


def place(block):
    return {"ctx": block // 2, "grp": block % 2}


def mm(a, b, dims):
    return lax.dot_general(a, b, dims, preferred_element_type=F32)


def kernel(devices, docs, heads, group, lens_ref, freq_ref, qgain_ref, kgain_ref, q_hbm, k_hbm, v_hbm, g_hbm,
           dq_ref, dk_ref, dv_ref, gains_ref,
           q, go, kv, dkv, term, back, cosd, sins, bias, q_rots, q_scales, k_rots, k_scales, box,
           load_sem, fs_sem, fr_sem, bs_sem, br_sem, as_sem, ar_sem, ready):
    me = lax.axis_index("ctx") * 2 + lax.axis_index("grp")
    slot_in_ring = me % RING
    ring = me // RING
    z = ring % ZS
    x = ring // ZS
    quad = z % 4
    zgroup = z // 4

    barrier = pltpu.get_barrier_semaphore()

    def greet(block):
        pl.semaphore_signal(barrier, inc=1, device_id=place(block), device_id_type=MESH)

    for hop in (1, 2):
        @pl.when(me >= hop)
        def _():
            greet(me - hop)

        @pl.when(me + hop < devices)
        def _():
            greet(me + hop)

    def ring_peer(i):
        return ring * RING + (slot_in_ring + i) % RING

    def quad_peer(i):
        return (x * ZS + zgroup * 4 + (quad + i) % 4) * RING + slot_in_ring

    def x_peer(i):
        return (((x + i) % XS) * ZS + z) * RING + slot_in_ring

    def group_peer(other):
        return (x * ZS + other * 4 + quad) * RING + slot_in_ring

    for i in range(1, RING):
        greet(ring_peer(i))

    for i in range(1, 4):
        greet(quad_peer(i))
        greet(x_peer(i))

    @pl.when(zgroup == 1)
    def _():
        greet(group_peer(0))
        greet(group_peer(2))

    @pl.when(zgroup != 1)
    def _():
        greet(group_peer(1))

    loads = [
        pltpu.make_async_copy(k_hbm, kv.at[0, 2], load_sem.at[0]),
        pltpu.make_async_copy(v_hbm, kv.at[1, 2], load_sem.at[1]),
        pltpu.make_async_copy(q_hbm, q, load_sem.at[2]),
        pltpu.make_async_copy(g_hbm, go, load_sem.at[3]),
    ]
    for load in loads:
        load.start()

    def columns(head):
        return pl.ds(pl.multiple_of(head * HEAD, HEAD), HEAD)

    def forward(hop, which, head):
        source = (k_hbm, v_hbm)[which]
        return pltpu.make_async_remote_copy(
            src_ref=source.at[:, columns(head)],
            dst_ref=kv.at[which, 2 - hop, :, columns(head)],
            send_sem=fs_sem.at[hop - 1, which, head],
            recv_sem=fr_sem.at[hop - 1, which, head],
            device_id=place(lax.rem(me + hop, devices)),
            device_id_type=MESH,
        )

    def backward(hop, which, head):
        return pltpu.make_async_remote_copy(
            src_ref=term.at[which, 2 - hop, :, columns(head)],
            dst_ref=back.at[which, hop - 1, :, columns(head)],
            send_sem=bs_sem.at[hop - 1, which, head],
            recv_sem=br_sem.at[hop - 1, which, head],
            device_id=place(lax.rem(me - hop + devices, devices)),
            device_id_type=MESH,
        )

    wide = -(-docs // 128) * 128
    lens = jnp.concatenate([lens_ref[...], jnp.zeros((1, wide - docs), jnp.int32)], 1).astype(F32)
    down = lax.broadcasted_iota(jnp.int32, (wide, wide), 0)
    along = lax.broadcasted_iota(jnp.int32, (wide, wide), 1)
    real_down = lax.broadcasted_iota(jnp.int32, (wide, 1), 0) < docs
    real_along = lax.broadcasted_iota(jnp.int32, (1, wide), 1) < docs
    lens_all = jnp.broadcast_to(lens, (wide, wide))
    lens_col = jnp.sum(jnp.where(down == along, lens_all, 0.0), axis=1, keepdims=True)
    ends_row = jnp.sum(jnp.where(down <= along, lens_col, 0.0), axis=0, keepdims=True)
    ends_col = jnp.sum(jnp.where(along <= down, lens_all, 0.0), axis=1, keepdims=True)
    ends_row = jnp.where(real_along, ends_row, 1e9)
    ends_col = jnp.where(real_down, ends_col, 1e9)
    first = (me - 2) * TOK
    key_tok = (first + lax.broadcasted_iota(jnp.int32, (KEYS, 1), 0)).astype(F32)
    own_tok = (first + WINDOW + lax.broadcasted_iota(jnp.int32, (1, TOK), 1)).astype(F32)
    key_before = ends_row <= key_tok
    key_start = jnp.max(jnp.where(key_before, ends_row, 0.0), axis=1, keepdims=True)
    key_doc = jnp.sum(jnp.where(key_before, 1.0, 0.0), axis=1, keepdims=True)
    own_doc = jnp.sum(jnp.where(ends_col <= own_tok, 1.0, 0.0), axis=0, keepdims=True)
    apart = own_tok - key_tok
    visible = (key_doc == own_doc) & (apart >= 0.0) & (apart < float(WINDOW)) & (key_tok >= 0.0)
    bias[...] = jnp.where(visible, 0.0, MASKED)
    near = (jnp.minimum(me, 1) + jnp.minimum(me // 2, 1)
            + jnp.minimum(devices - 1 - me, 1) + jnp.minimum((devices - 1 - me) // 2, 1))
    pl.semaphore_wait(barrier, near + (RING - 1) + 3 + 3 + 1 + (zgroup % 2))

    @pl.when(zgroup == 1)
    def _():
        for other in (0, 2):
            pl.semaphore_signal(ready, inc=1, device_id=place(group_peer(other)), device_id_type=MESH)

    def send_keys(head):
        for hop in (1, 2):
            @pl.when(me + hop < devices)
            def _():
                for which in (0, 1):
                    forward(hop, which, head).start()

    def send_terms(head):
        for hop in (1, 2):
            @pl.when(me >= hop)
            def _():
                for which in (0, 1):
                    backward(hop, which, head).start()

    for head in range(AHEAD):
        send_keys(head)

    for hop in (1, 2):
        @pl.when(me < hop)
        def _():
            kv[:, 2 - hop] = jnp.zeros((2, TOK, heads * HEAD), BF16)

        @pl.when(me + hop >= devices)
        def _():
            back[:, hop - 1] = jnp.zeros((2, TOK, heads * HEAD), BF16)

    angle = (key_tok - key_start) * freq_ref[...]
    cosd[...] = jnp.cos(angle)
    front = lax.broadcasted_iota(jnp.int32, (1, HEAD), 1) < HALF
    sine = jnp.sin(angle)
    sins[...] = jnp.where(front, -sine, sine)

    for load in loads:
        load.wait()

    kgain = kgain_ref[...]
    qgain = qgain_ref[...]
    own = pl.ds(WINDOW, TOK)

    share = jnp.full((HEAD, HEAD), 1.0 / HEAD, BF16)

    def mean(values):
        high = values.astype(BF16)
        low = (values - high.astype(F32)).astype(BF16)
        return mm(high, share, NN) + mm(low, share, NN)

    def scale_of(values):
        return lax.rsqrt(mean(values * values) + EPS)

    def rotate(normed, cosine, sine):
        return normed * cosine + pltpu.roll(normed, HALF, 1) * sine

    def unrotate(grads, cosine, sine):
        return grads * cosine - pltpu.roll(grads, HALF, 1) * sine

    def raw_grad(grad_normed, unit, scale, gain):
        weighted = grad_normed * gain
        return scale * (weighted - unit * mean(weighted * unit))

    @pl.loop(0, heads)
    def _(head):
        cosine, sine = cosd[own, :], sins[own, :]
        raw = kv[0, 2, :, columns(head)].astype(F32)
        scale = scale_of(raw)
        k_scales[head] = scale
        k_rots[head] = rotate(raw * scale * kgain, cosine, sine).astype(BF16)
        for i in range(group):
            raw = q[:, columns(head * group + i)].astype(F32)
            scale = scale_of(raw)
            q_scales[head, pl.ds(i * TOK, TOK), :] = scale
            q_rots[head, pl.ds(i * TOK, TOK), :] = rotate(raw * scale * qgain, cosine, sine).astype(BF16)

    def head_step(head, sums):
        q_sum, k_sum = sums
        for hop in (1, 2):
            @pl.when((me + hop < devices) & (head + AHEAD < heads))
            def _():
                for which in (0, 1):
                    forward(hop, which, head).wait_send()
                for which in (0, 1):
                    forward(hop, which, head + AHEAD).start()

        for hop in (1, 2):
            @pl.when(me >= hop)
            def _():
                for which in (0, 1):
                    forward(hop, which, head).wait_recv()

        cols = columns(head)
        keys = kv[0, :2, :, cols].reshape(WINDOW, HEAD).astype(F32)
        values = kv[1, :, :, cols].reshape(KEYS, HEAD)
        k_unit = keys * scale_of(keys)
        past = pl.ds(0, WINDOW)
        k_rot = jnp.concatenate([rotate(k_unit * kgain, cosd[past, :], sins[past, :]).astype(BF16), k_rots[head]], 0)
        k_unit = jnp.concatenate([k_unit, kv[0, 2, :, cols].astype(F32) * k_scales[head]], 0)
        q_cols = [columns(head * group + i) for i in range(group)]
        q_rot = q_rots[head]
        g_out = jnp.concatenate([go[:, c] for c in q_cols], 0)
        masks = jnp.concatenate([bias[...]] * group, 1)
        scores = mm(k_rot, q_rot, NT) + masks
        prob_grad = mm(values, g_out, NT)
        top = jnp.max(scores, axis=0, keepdims=True)
        exps = jnp.exp2((scores - top) * (SCALE * LOG2E))
        probs = exps * (1.0 / jnp.sum(exps, axis=0, keepdims=True))
        delta = jnp.sum(probs * prob_grad, axis=0, keepdims=True)
        score_grad = (probs * (prob_grad - delta)).astype(BF16)
        v_term = mm(probs.astype(BF16), g_out, NN)
        k_term = mm(score_grad, q_rot, NN) * SCALE
        q_term = mm(score_grad, k_rot, TN) * SCALE
        v_far = v_term[:WINDOW].astype(BF16)
        k_far = k_term[:WINDOW].astype(BF16)
        term[0, :, :, cols] = k_far.reshape(2, TOK, HEAD)
        term[1, :, :, cols] = v_far.reshape(2, TOK, HEAD)
        dkv[0, :, cols] = k_term[WINDOW:]
        dkv[1, :, cols] = v_term[WINDOW:]
        k_all = jnp.concatenate([k_far.astype(F32), k_term[WINDOW:]], 0)
        k_sum = k_sum + jnp.sum(unrotate(k_all, cosd[...], sins[...]) * k_unit, axis=0, keepdims=True)
        for i, c in enumerate(q_cols):
            scale = q_scales[head, pl.ds(i * TOK, TOK), :]
            unit = q[:, c].astype(F32) * scale
            normed = unrotate(q_term[i * TOK:(i + 1) * TOK], cosd[own, :], sins[own, :])
            q_sum = q_sum + jnp.sum(normed * unit, axis=0, keepdims=True)
            dq_ref[:, c] = raw_grad(normed, unit, scale, qgain).astype(BF16)

        for hop in (1, 2):
            @pl.when((me >= hop) & (head >= HOLD))
            def _():
                for which in (0, 1):
                    backward(hop, which, head - HOLD).start()

        return q_sum, k_sum

    zero = jnp.zeros((1, HEAD), F32)
    q_sum, k_sum = lax.fori_loop(0, heads, head_step, (zero, zero))

    row = lax.broadcasted_iota(jnp.int32, (8, HEAD), 0)
    part = jnp.where(row == 0, q_sum, jnp.where(row == 1, k_sum, 0.0))

    def message(source, target, index, peer, sem):
        return pltpu.make_async_remote_copy(
            src_ref=source, dst_ref=target, send_sem=as_sem.at[index], recv_sem=ar_sem.at[sem],
            device_id=place(peer), device_id_type=MESH,
        )

    def summed(values):
        out = values[0]
        for value in values[1:]:
            out = out + value
        return out

    pending = []

    def launch(part, base, count, mine, peer):
        box[base + mine] = part
        for i in range(1, count):
            copy = message(box.at[base + mine], box.at[base + mine], base + i, peer(i), base + mine)
            copy.start()
            pending.append(copy)

    def collect(base, count, mine, peer):
        for i in range(1, count):
            there = base + (mine + i) % count
            message(box.at[there], box.at[there], base + i, peer(i), there).wait_recv()
        return summed([box[base + i] for i in range(count)])

    launch(part, 0, RING, slot_in_ring, ring_peer)
    for head in range(heads - HOLD, heads - HOLD + 1):
        send_terms(head)
    part = collect(0, RING, slot_in_ring, ring_peer)
    launch(part, RING, XS, x, x_peer)
    for head in range(heads - HOLD + 1, heads - HOLD + 2):
        send_terms(head)
    part = collect(RING, XS, x, x_peer)
    launch(part, RING + XS, 4, quad, quad_peer)
    for head in range(heads - HOLD + 2, heads - HOLD + 3):
        send_terms(head)
    part = collect(RING + XS, 4, quad, quad_peer)
    last = RING + XS + 4

    def far_peer(i):
        return group_peer((zgroup + i) % 3)

    @pl.when(zgroup != 1)
    def _():
        pl.semaphore_wait(ready, 1)

    launch(part, last, 3, zgroup, far_peer)
    for head in range(heads - HOLD + 3, heads):
        send_terms(head)

    @pl.loop(0, heads)
    def _(head):
        for hop in (1, 2):
            @pl.when(me + hop < devices)
            def _():
                for which in (0, 1):
                    backward(hop, which, head).wait_recv()

        cols = columns(head)
        k_grad = dkv[0, :, cols] + back[0, 0, :, cols].astype(F32) + back[0, 1, :, cols].astype(F32)
        v_grad = dkv[1, :, cols] + back[1, 0, :, cols].astype(F32) + back[1, 1, :, cols].astype(F32)
        dv_ref[:, cols] = v_grad.astype(BF16)
        scale = k_scales[head]
        unit = kv[0, 2, :, cols].astype(F32) * scale
        normed = unrotate(k_grad, cosd[own, :], sins[own, :])
        dk_ref[:, cols] = raw_grad(normed, unit, scale, kgain).astype(BF16)

    gains_ref[...] = collect(last, 3, zgroup, far_peer)
    for copy in pending:
        copy.wait_send()

    for hop in (1, 2):
        @pl.when(me + hop < devices)
        def _():
            for head in range(heads - AHEAD, heads):
                for which in (0, 1):
                    forward(hop, which, head).wait_send()

        @pl.when(me >= hop)
        def _():
            for head in range(heads):
                for which in (0, 1):
                    backward(hop, which, head).wait_send()


def finish(dq_in, dk_in, dv_in, gains_in, dq, dk, dv, q_gain, k_gain, sems):
    copies = [
        pltpu.make_async_copy(dq_in, dq, sems.at[0]),
        pltpu.make_async_copy(dk_in, dk, sems.at[1]),
        pltpu.make_async_copy(dv_in, dv, sems.at[2]),
    ]
    for copy in copies:
        copy.start()
    q_gain[...] = gains_in[0:1, :]
    k_gain[...] = gains_in[1:2, :]
    for copy in copies:
        copy.wait()


def on_device(devices, doc_lengths, query_raw, key_raw, value_matrix, out_grad, query_gain, key_gain):
    heads = key_raw.shape[1] // HEAD
    group = query_raw.shape[1] // key_raw.shape[1]
    docs = doc_lengths.shape[0]
    lens = doc_lengths.reshape(1, docs)
    lane = np.arange(HEAD) % HALF
    freq = jnp.asarray((np.float64(BASE) ** (-2.0 * lane / HEAD)).astype(np.float32).reshape(1, HEAD))
    vmem = pl.BlockSpec(memory_space=pltpu.VMEM)
    anywhere = pl.BlockSpec(memory_space=pl.ANY)
    width = heads * HEAD
    grad_query, grad_key, grad_value, gains = pl.pallas_call(
        functools.partial(kernel, devices, docs, heads, group),
        out_shape=(
            jax.ShapeDtypeStruct(query_raw.shape, BF16),
            jax.ShapeDtypeStruct(key_raw.shape, BF16),
            jax.ShapeDtypeStruct(key_raw.shape, BF16),
            jax.ShapeDtypeStruct((8, HEAD), F32),
        ),
        in_specs=[vmem] * 4 + [anywhere] * 4,
        out_specs=(vmem, vmem, vmem, vmem),
        scratch_shapes=[
            pltpu.VMEM((TOK, width * group), BF16),
            pltpu.VMEM((TOK, width * group), BF16),
            pltpu.VMEM((2, 3, TOK, width), BF16),
            pltpu.VMEM((2, TOK, width), F32),
            pltpu.VMEM((2, 2, TOK, width), BF16),
            pltpu.VMEM((2, 2, TOK, width), BF16),
            pltpu.VMEM((KEYS, HEAD), F32),
            pltpu.VMEM((KEYS, HEAD), F32),
            pltpu.VMEM((KEYS, HEAD), F32),
            pltpu.VMEM((heads, group * TOK, HEAD), BF16),
            pltpu.VMEM((heads, group * TOK, HEAD), F32),
            pltpu.VMEM((heads, TOK, HEAD), BF16),
            pltpu.VMEM((heads, TOK, HEAD), F32),
            pltpu.VMEM((RING + XS + 4 + 3, 8, HEAD), F32),
            pltpu.SemaphoreType.DMA((4,)),
            pltpu.SemaphoreType.DMA((2, 2, heads)),
            pltpu.SemaphoreType.DMA((2, 2, heads)),
            pltpu.SemaphoreType.DMA((2, 2, heads)),
            pltpu.SemaphoreType.DMA((2, 2, heads)),
            pltpu.SemaphoreType.DMA((RING + XS + 4 + 3,)),
            pltpu.SemaphoreType.DMA((RING + XS + 4 + 3,)),
            pltpu.SemaphoreType.REGULAR,
        ],
        compiler_params=pltpu.CompilerParams(
            collective_id=0, has_side_effects=True, vmem_limit_bytes=56 << 20
        ),
    )(lens, freq, query_gain.reshape(1, HEAD), key_gain.reshape(1, HEAD), query_raw, key_raw, value_matrix, out_grad)
    grad_query, grad_key, grad_value, q_gain, k_gain = pl.pallas_call(
        finish,
        out_shape=(
            jax.ShapeDtypeStruct(query_raw.shape, BF16),
            jax.ShapeDtypeStruct(key_raw.shape, BF16),
            jax.ShapeDtypeStruct(key_raw.shape, BF16),
            jax.ShapeDtypeStruct((1, HEAD), F32),
            jax.ShapeDtypeStruct((1, HEAD), F32),
        ),
        in_specs=[vmem] * 4,
        out_specs=(anywhere, anywhere, anywhere, vmem, vmem),
        scratch_shapes=[pltpu.SemaphoreType.DMA((3,))],
    )(grad_query, grad_key, grad_value, gains)
    return grad_query, grad_key, grad_value, q_gain.reshape(HEAD), k_gain.reshape(HEAD)


def solution(mesh):
    devices = mesh.devices.size
    rows = P(("ctx", "grp"), None)
    return jax.shard_map(
        functools.partial(on_device, devices),
        mesh=mesh,
        in_specs=(P(), rows, rows, rows, rows, P(), P()),
        out_specs=(rows, rows, rows, P(), P()),
        check_vma=False,
    )
```

```python
import functools

import jax
import jax.numpy as jnp
import numpy as np
from jax import lax
from jax.experimental import pallas as pl
from jax.experimental.pallas import tpu as pltpu
from jax.sharding import PartitionSpec as P

HEAD = 128
HALF = HEAD // 2
WINDOW = 256
TOK = 128
KEYS = WINDOW + TOK
EPS = 1e-06
SCALE = 168.0 ** (-0.5)
BASE = 10000.0
MASKED = -1e30
LOG2E = 1.4426950408889634
HOLD = 4
RING = 16
ZS = 12
XS = 4
MESH = pl.DeviceIdType.MESH
F32 = jnp.float32
BF16 = jnp.bfloat16
NT = (((1,), (1,)), ((), ()))
NN = (((1,), (0,)), ((), ()))
TN = (((0,), (0,)), ((), ()))


def place(block):
    return {"ctx": block // 2, "grp": block % 2}


def mm(a, b, dims):
    return lax.dot_general(a, b, dims, preferred_element_type=F32)


def kernel(devices, docs, heads, group, lens_ref, freq_ref, qgain_ref, kgain_ref, q_hbm, k_hbm, v_hbm, g_hbm,
           dq_hbm, dk_hbm, dv_hbm, gains_ref,
           dq_ref, dk_ref, dv_ref, q, go, kv, dkv, term, back, cosd, sins, bias, q_rots, q_scales, k_rots, k_scales, box,
           load_sem, fs_sem, fr_sem, bs_sem, br_sem, as_sem, ar_sem, out_sem, ready):
    me = lax.axis_index("ctx") * 2 + lax.axis_index("grp")
    slot_in_ring = me % RING
    ring = me // RING
    z = ring % ZS
    x = ring // ZS
    quad = z % 4
    zgroup = z // 4

    barrier = pltpu.get_barrier_semaphore()

    def greet(block):
        pl.semaphore_signal(barrier, inc=1, device_id=place(block), device_id_type=MESH)

    for hop in (1, 2):
        @pl.when(me >= hop)
        def _():
            greet(me - hop)

        @pl.when(me + hop < devices)
        def _():
            greet(me + hop)

    def ring_peer(i):
        return ring * RING + (slot_in_ring + i) % RING

    def quad_peer(i):
        return (x * ZS + zgroup * 4 + (quad + i) % 4) * RING + slot_in_ring

    def x_peer(i):
        return (((x + i) % XS) * ZS + z) * RING + slot_in_ring

    def group_peer(other):
        return (x * ZS + other * 4 + quad) * RING + slot_in_ring

    for i in range(1, RING):
        greet(ring_peer(i))

    for i in range(1, 4):
        greet(quad_peer(i))
        greet(x_peer(i))

    @pl.when(zgroup == 1)
    def _():
        greet(group_peer(0))
        greet(group_peer(2))

    @pl.when(zgroup != 1)
    def _():
        greet(group_peer(1))

    loads = [
        pltpu.make_async_copy(k_hbm, kv.at[0, 2], load_sem.at[0]),
        pltpu.make_async_copy(v_hbm, kv.at[1, 2], load_sem.at[1]),
        pltpu.make_async_copy(q_hbm, q, load_sem.at[2]),
        pltpu.make_async_copy(g_hbm, go, load_sem.at[3]),
    ]
    for load in loads:
        load.start()

    def columns(head):
        return pl.ds(pl.multiple_of(head * HEAD, HEAD), HEAD)

    def forward(hop, which, head):
        source = (k_hbm, v_hbm)[which]
        return pltpu.make_async_remote_copy(
            src_ref=source.at[:, columns(head)],
            dst_ref=kv.at[which, 2 - hop, :, columns(head)],
            send_sem=fs_sem.at[hop - 1, which, head],
            recv_sem=fr_sem.at[hop - 1, which, head],
            device_id=place(lax.rem(me + hop, devices)),
            device_id_type=MESH,
        )

    def backward(hop, which, head):
        return pltpu.make_async_remote_copy(
            src_ref=term.at[which, 2 - hop, :, columns(head)],
            dst_ref=back.at[which, hop - 1, :, columns(head)],
            send_sem=bs_sem.at[hop - 1, which, head],
            recv_sem=br_sem.at[hop - 1, which, head],
            device_id=place(lax.rem(me - hop + devices, devices)),
            device_id_type=MESH,
        )

    near = (jnp.minimum(me, 1) + jnp.minimum(me // 2, 1)
            + jnp.minimum(devices - 1 - me, 1) + jnp.minimum((devices - 1 - me) // 2, 1))
    pl.semaphore_wait(barrier, near + (RING - 1) + 3 + 3 + 1 + (zgroup % 2))

    @pl.when(zgroup == 1)
    def _():
        for other in (0, 2):
            pl.semaphore_signal(ready, inc=1, device_id=place(group_peer(other)), device_id_type=MESH)

    def send_keys(head):
        for hop in (1, 2):
            @pl.when(me + hop < devices)
            def _():
                for which in (0, 1):
                    forward(hop, which, head).start()

    def send_terms(head):
        for hop in (1, 2):
            @pl.when(me >= hop)
            def _():
                for which in (0, 1):
                    backward(hop, which, head).start()

    @pl.loop(0, heads)
    def _(head):
        send_keys(head)

    for hop in (1, 2):
        @pl.when(me < hop)
        def _():
            kv[:, 2 - hop] = jnp.zeros((2, TOK, heads * HEAD), BF16)

        @pl.when(me + hop >= devices)
        def _():
            back[:, hop - 1] = jnp.zeros((2, TOK, heads * HEAD), BF16)

    wide = -(-docs // 128) * 128
    lens = jnp.concatenate([lens_ref[...], jnp.zeros((1, wide - docs), jnp.int32)], 1).astype(F32)
    down = lax.broadcasted_iota(jnp.int32, (wide, wide), 0)
    along = lax.broadcasted_iota(jnp.int32, (wide, wide), 1)
    real_down = lax.broadcasted_iota(jnp.int32, (wide, 1), 0) < docs
    real_along = lax.broadcasted_iota(jnp.int32, (1, wide), 1) < docs
    lens_all = jnp.broadcast_to(lens, (wide, wide))
    lens_col = jnp.sum(jnp.where(down == along, lens_all, 0.0), axis=1, keepdims=True)
    ends_row = jnp.sum(jnp.where(down <= along, lens_col, 0.0), axis=0, keepdims=True)
    ends_col = jnp.sum(jnp.where(along <= down, lens_all, 0.0), axis=1, keepdims=True)
    ends_row = jnp.where(real_along, ends_row, 1e9)
    ends_col = jnp.where(real_down, ends_col, 1e9)
    first = (me - 2) * TOK
    key_tok = (first + lax.broadcasted_iota(jnp.int32, (KEYS, 1), 0)).astype(F32)
    own_tok = (first + WINDOW + lax.broadcasted_iota(jnp.int32, (1, TOK), 1)).astype(F32)
    key_before = ends_row <= key_tok
    key_start = jnp.max(jnp.where(key_before, ends_row, 0.0), axis=1, keepdims=True)
    key_doc = jnp.sum(jnp.where(key_before, 1.0, 0.0), axis=1, keepdims=True)
    own_doc = jnp.sum(jnp.where(ends_col <= own_tok, 1.0, 0.0), axis=0, keepdims=True)
    apart = own_tok - key_tok
    visible = (key_doc == own_doc) & (apart >= 0.0) & (apart < float(WINDOW)) & (key_tok >= 0.0)
    bias[...] = jnp.where(visible, 0.0, MASKED)
    angle = (key_tok - key_start) * freq_ref[...]
    cosd[...] = jnp.cos(angle)
    front = lax.broadcasted_iota(jnp.int32, (1, HEAD), 1) < HALF
    sine = jnp.sin(angle)
    sins[...] = jnp.where(front, -sine, sine)

    for load in loads:
        load.wait()

    kgain = kgain_ref[...]
    qgain = qgain_ref[...]
    own = pl.ds(WINDOW, TOK)

    share = jnp.full((HEAD, HEAD), 1.0 / HEAD, BF16)

    def mean(values):
        high = values.astype(BF16)
        low = (values - high.astype(F32)).astype(BF16)
        return mm(high, share, NN) + mm(low, share, NN)

    def scale_of(values):
        return lax.rsqrt(mean(values * values) + EPS)

    def rotate(normed, cosine, sine):
        return normed * cosine + pltpu.roll(normed, HALF, 1) * sine

    def unrotate(grads, cosine, sine):
        return grads * cosine - pltpu.roll(grads, HALF, 1) * sine

    def raw_grad(grad_normed, unit, scale, gain):
        weighted = grad_normed * gain
        return scale * (weighted - unit * mean(weighted * unit))

    @pl.loop(0, heads)
    def _(head):
        cosine, sine = cosd[own, :], sins[own, :]
        raw = kv[0, 2, :, columns(head)].astype(F32)
        scale = scale_of(raw)
        k_scales[head] = scale
        k_rots[head] = rotate(raw * scale * kgain, cosine, sine).astype(BF16)
        for i in range(group):
            raw = q[:, columns(head * group + i)].astype(F32)
            scale = scale_of(raw)
            q_scales[head, pl.ds(i * TOK, TOK), :] = scale
            q_rots[head, pl.ds(i * TOK, TOK), :] = rotate(raw * scale * qgain, cosine, sine).astype(BF16)

    hold = HOLD

    def head_step(head, sums):
        q_sum, k_sum = sums
        for hop in (1, 2):
            @pl.when(me >= hop)
            def _():
                for which in (0, 1):
                    forward(hop, which, head).wait_recv()

        cols = columns(head)
        keys = kv[0, :2, :, cols].reshape(WINDOW, HEAD).astype(F32)
        values = kv[1, :, :, cols].reshape(KEYS, HEAD)
        k_unit = keys * scale_of(keys)
        past = pl.ds(0, WINDOW)
        k_rot = jnp.concatenate([rotate(k_unit * kgain, cosd[past, :], sins[past, :]).astype(BF16), k_rots[head]], 0)
        k_unit = jnp.concatenate([k_unit, kv[0, 2, :, cols].astype(F32) * k_scales[head]], 0)
        q_cols = [columns(head * group + i) for i in range(group)]
        q_rot = q_rots[head]
        g_out = jnp.concatenate([go[:, c] for c in q_cols], 0)
        masks = jnp.concatenate([bias[...]] * group, 1)
        scores = mm(k_rot, q_rot, NT) + masks
        prob_grad = mm(values, g_out, NT)
        top = jnp.max(scores, axis=0, keepdims=True)
        exps = jnp.exp2((scores - top) * (SCALE * LOG2E))
        probs = exps * (1.0 / jnp.sum(exps, axis=0, keepdims=True))
        delta = jnp.sum(probs * prob_grad, axis=0, keepdims=True)
        score_grad = (probs * (prob_grad - delta)).astype(BF16)
        v_term = mm(probs.astype(BF16), g_out, NN)
        k_term = mm(score_grad, q_rot, NN) * SCALE
        q_term = mm(score_grad, k_rot, TN) * SCALE
        v_far = v_term[:WINDOW].astype(BF16)
        k_far = k_term[:WINDOW].astype(BF16)
        term[0, :, :, cols] = k_far.reshape(2, TOK, HEAD)
        term[1, :, :, cols] = v_far.reshape(2, TOK, HEAD)
        dkv[0, :, cols] = k_term[WINDOW:]
        dkv[1, :, cols] = v_term[WINDOW:]
        k_all = jnp.concatenate([k_far.astype(F32), k_term[WINDOW:]], 0)
        k_sum = k_sum + jnp.sum(unrotate(k_all, cosd[...], sins[...]) * k_unit, axis=0, keepdims=True)
        for i, c in enumerate(q_cols):
            scale = q_scales[head, pl.ds(i * TOK, TOK), :]
            unit = q[:, c].astype(F32) * scale
            normed = unrotate(q_term[i * TOK:(i + 1) * TOK], cosd[own, :], sins[own, :])
            q_sum = q_sum + jnp.sum(normed * unit, axis=0, keepdims=True)
            dq_ref[:, c] = raw_grad(normed, unit, scale, qgain).astype(BF16)

        for hop in (1, 2):
            @pl.when((me >= hop) & (head >= hold))
            def _():
                for which in (0, 1):
                    backward(hop, which, head - hold).start()

        return q_sum, k_sum

    zero = jnp.zeros((1, HEAD), F32)
    q_sum, k_sum = lax.fori_loop(0, heads, head_step, (zero, zero))

    part = jnp.concatenate([q_sum, k_sum], 0)

    def message(source, target, index, peer, sem):
        return pltpu.make_async_remote_copy(
            src_ref=source, dst_ref=target, send_sem=as_sem.at[index], recv_sem=ar_sem.at[sem],
            device_id=place(peer), device_id_type=MESH,
        )

    def summed(values):
        out = values[0]
        for value in values[1:]:
            out = out + value
        return out

    pending = []

    def launch(part, base, count, mine, peer):
        box[base + mine] = part
        for i in range(1, count):
            copy = message(box.at[base + mine], box.at[base + mine], base + i, peer(i), base + mine)
            copy.start()
            pending.append(copy)

    def collect(base, count, mine, peer):
        for i in range(1, count):
            there = base + (mine + i) % count
            message(box.at[there], box.at[there], base + i, peer(i), there).wait_recv()
        return summed([box[base + i] for i in range(count)])

    dq_copy = pltpu.make_async_copy(dq_ref, dq_hbm, out_sem.at[0])
    launch(part, 0, RING, slot_in_ring, ring_peer)
    dq_copy.start()
    send_terms(heads - hold)
    part = collect(0, RING, slot_in_ring, ring_peer)
    launch(part, RING, XS, x, x_peer)
    send_terms(heads - hold + 1)
    part = collect(RING, XS, x, x_peer)
    launch(part, RING + XS, 4, quad, quad_peer)
    send_terms(heads - hold + 2)
    part = collect(RING + XS, 4, quad, quad_peer)
    last = RING + XS + 4

    def far_peer(i):
        return group_peer((zgroup + i) % 3)

    @pl.when(zgroup != 1)
    def _():
        pl.semaphore_wait(ready, 1)

    launch(part, last, 3, zgroup, far_peer)

    @pl.loop(heads - hold + 3, heads)
    def _(head):
        send_terms(head)

    @pl.loop(0, heads)
    def _(head):
        for hop in (1, 2):
            @pl.when(me + hop < devices)
            def _():
                for which in (0, 1):
                    backward(hop, which, head).wait_recv()

        cols = columns(head)
        k_grad = dkv[0, :, cols] + back[0, 0, :, cols].astype(F32) + back[0, 1, :, cols].astype(F32)
        v_grad = dkv[1, :, cols] + back[1, 0, :, cols].astype(F32) + back[1, 1, :, cols].astype(F32)
        dv_ref[:, cols] = v_grad.astype(BF16)
        scale = k_scales[head]
        unit = kv[0, 2, :, cols].astype(F32) * scale
        normed = unrotate(k_grad, cosd[own, :], sins[own, :])
        dk_ref[:, cols] = raw_grad(normed, unit, scale, kgain).astype(BF16)

    outs = [pltpu.make_async_copy(dk_ref, dk_hbm, out_sem.at[1]), pltpu.make_async_copy(dv_ref, dv_hbm, out_sem.at[2])]
    for out in outs:
        out.start()
    gains_ref[...] = collect(last, 3, zgroup, far_peer)
    for copy in pending:
        copy.wait_send()
    dq_copy.wait()
    for out in outs:
        out.wait()

    for hop in (1, 2):
        @pl.when(me + hop < devices)
        def _():
            for head in range(heads):
                for which in (0, 1):
                    forward(hop, which, head).wait_send()

        @pl.when(me >= hop)
        def _():
            for head in range(heads):
                for which in (0, 1):
                    backward(hop, which, head).wait_send()


def finish(dq_in, dk_in, dv_in, gains_in, dq, dk, dv, q_gain, k_gain, sems):
    copies = [
        pltpu.make_async_copy(dq_in, dq, sems.at[0]),
        pltpu.make_async_copy(dk_in, dk, sems.at[1]),
        pltpu.make_async_copy(dv_in, dv, sems.at[2]),
    ]
    for copy in copies:
        copy.start()
    q_gain[...] = gains_in[0:1, :]
    k_gain[...] = gains_in[1:2, :]
    for copy in copies:
        copy.wait()


def on_device(devices, doc_lengths, query_raw, key_raw, value_matrix, out_grad, query_gain, key_gain):
    heads = key_raw.shape[1] // HEAD
    group = query_raw.shape[1] // key_raw.shape[1]
    docs = doc_lengths.shape[0]
    lens = doc_lengths.reshape(1, docs)
    lane = np.arange(HEAD) % HALF
    freq = jnp.asarray((np.float64(BASE) ** (-2.0 * lane / HEAD)).astype(np.float32).reshape(1, HEAD))
    vmem = pl.BlockSpec(memory_space=pltpu.VMEM)
    anywhere = pl.BlockSpec(memory_space=pl.ANY)
    width = heads * HEAD
    grad_query, grad_key, grad_value, gains = pl.pallas_call(
        functools.partial(kernel, devices, docs, heads, group),
        out_shape=(
            jax.ShapeDtypeStruct(query_raw.shape, BF16),
            jax.ShapeDtypeStruct(key_raw.shape, BF16),
            jax.ShapeDtypeStruct(key_raw.shape, BF16),
            jax.ShapeDtypeStruct((2, HEAD), F32),
        ),
        in_specs=[vmem] * 4 + [anywhere] * 4,
        out_specs=(anywhere, anywhere, anywhere, vmem),
        scratch_shapes=[
            pltpu.VMEM((TOK, width * group), BF16),
            pltpu.VMEM((TOK, width), BF16),
            pltpu.VMEM((TOK, width), BF16),
            pltpu.VMEM((TOK, width * group), BF16),
            pltpu.VMEM((TOK, width * group), BF16),
            pltpu.VMEM((2, 3, TOK, width), BF16),
            pltpu.VMEM((2, TOK, width), F32),
            pltpu.VMEM((2, 2, TOK, width), BF16),
            pltpu.VMEM((2, 2, TOK, width), BF16),
            pltpu.VMEM((KEYS, HEAD), F32),
            pltpu.VMEM((KEYS, HEAD), F32),
            pltpu.VMEM((KEYS, HEAD), F32),
            pltpu.VMEM((heads, group * TOK, HEAD), BF16),
            pltpu.VMEM((heads, group * TOK, HEAD), F32),
            pltpu.VMEM((heads, TOK, HEAD), BF16),
            pltpu.VMEM((heads, TOK, HEAD), F32),
            pltpu.VMEM((RING + XS + 4 + 3, 2, HEAD), F32),
            pltpu.SemaphoreType.DMA((4,)),
            pltpu.SemaphoreType.DMA((2, 2, heads)),
            pltpu.SemaphoreType.DMA((2, 2, heads)),
            pltpu.SemaphoreType.DMA((2, 2, heads)),
            pltpu.SemaphoreType.DMA((2, 2, heads)),
            pltpu.SemaphoreType.DMA((RING + XS + 4 + 3,)),
            pltpu.SemaphoreType.DMA((RING + XS + 4 + 3,)),
            pltpu.SemaphoreType.DMA((3,)),
            pltpu.SemaphoreType.REGULAR,
        ],
        compiler_params=pltpu.CompilerParams(
            collective_id=0, has_side_effects=True, vmem_limit_bytes=56 << 20
        ),
    )(lens, freq, query_gain.reshape(1, HEAD), key_gain.reshape(1, HEAD), query_raw, key_raw, value_matrix, out_grad)
    grad_query, grad_key, grad_value, q_gain, k_gain = pl.pallas_call(
        finish,
        out_shape=(
            jax.ShapeDtypeStruct(query_raw.shape, BF16),
            jax.ShapeDtypeStruct(key_raw.shape, BF16),
            jax.ShapeDtypeStruct(key_raw.shape, BF16),
            jax.ShapeDtypeStruct((1, HEAD), F32),
            jax.ShapeDtypeStruct((1, HEAD), F32),
        ),
        in_specs=[vmem] * 4,
        out_specs=(anywhere, anywhere, anywhere, vmem, vmem),
        scratch_shapes=[pltpu.SemaphoreType.DMA((3,))],
    )(grad_query, grad_key, grad_value, gains)
    return grad_query, grad_key, grad_value, q_gain.reshape(HEAD), k_gain.reshape(HEAD)


def solution(mesh):
    devices = mesh.devices.size
    rows = P(("ctx", "grp"), None)
    return jax.shard_map(
        functools.partial(on_device, devices),
        mesh=mesh,
        in_specs=(P(), rows, rows, rows, rows, P(), P()),
        out_specs=(rows, rows, rows, P(), P()),
        check_vma=False,
    )
```

```python
import functools

import jax
import jax.numpy as jnp
import numpy as np
from jax import lax
from jax.experimental import pallas as pl
from jax.experimental.pallas import tpu as pltpu
from jax.sharding import PartitionSpec as P

HEAD = 128
HALF = HEAD // 2
WINDOW = 256
TOK = 128
KEYS = WINDOW + TOK
EPS = 1e-06
SCALE = 168.0 ** (-0.5)
BASE = 10000.0
MASKED = -1e30
LOG2E = 1.4426950408889634
HOLD = 4
RING = 16
ZS = 12
NEAR = 16
MESH = pl.DeviceIdType.MESH
F32 = jnp.float32
BF16 = jnp.bfloat16
NT = (((1,), (1,)), ((), ()))
NN = (((1,), (0,)), ((), ()))
TN = (((0,), (0,)), ((), ()))


def place(block):
    return {"ctx": block // 2, "grp": block % 2}


def mm(a, b, dims):
    return lax.dot_general(a, b, dims, preferred_element_type=F32)


def kernel(devices, docs, heads, group, lens_ref, freq_ref, qgain_ref, kgain_ref, q_hbm, k_hbm, v_hbm, g_hbm,
           dq_hbm, dk_hbm, dv_hbm, gains_ref,
           dq_ref, dk_ref, dv_ref, q, go, kv, dkv, term, back, cosd, sins, bias, q_rots, q_scales, k_rots, k_scales, box,
           load_sem, fs_sem, fr_sem, bs_sem, br_sem, as_sem, ar_sem, out_sem, ready):
    me = lax.axis_index("ctx") * 2 + lax.axis_index("grp")
    slot_in_ring = me % RING
    ring = me // RING
    z = ring % ZS
    x = ring // ZS
    quad = z % 4
    zgroup = z // 4

    barrier = pltpu.get_barrier_semaphore()

    def greet(block):
        pl.semaphore_signal(barrier, inc=1, device_id=place(block), device_id_type=MESH)

    for hop in (1, 2):
        @pl.when(me >= hop)
        def _():
            greet(me - hop)

        @pl.when(me + hop < devices)
        def _():
            greet(me + hop)

    def ring_peer(i):
        return ring * RING + (slot_in_ring + i) % RING

    near_slot = x * 4 + quad

    def near_peer(i):
        there = (near_slot + i) % NEAR
        return ((there // 4) * ZS + zgroup * 4 + there % 4) * RING + slot_in_ring

    def group_peer(other):
        return (x * ZS + other * 4 + quad) * RING + slot_in_ring

    for i in range(1, RING):
        greet(ring_peer(i))

    for i in range(1, NEAR):
        greet(near_peer(i))

    @pl.when(zgroup == 1)
    def _():
        greet(group_peer(0))
        greet(group_peer(2))

    @pl.when(zgroup != 1)
    def _():
        greet(group_peer(1))

    loads = [
        pltpu.make_async_copy(k_hbm, kv.at[0, 2], load_sem.at[0]),
        pltpu.make_async_copy(v_hbm, kv.at[1, 2], load_sem.at[1]),
        pltpu.make_async_copy(q_hbm, q, load_sem.at[2]),
        pltpu.make_async_copy(g_hbm, go, load_sem.at[3]),
    ]
    for load in loads:
        load.start()

    def columns(head):
        return pl.ds(pl.multiple_of(head * HEAD, HEAD), HEAD)

    def forward(hop, which, head):
        source = (k_hbm, v_hbm)[which]
        return pltpu.make_async_remote_copy(
            src_ref=source.at[:, columns(head)],
            dst_ref=kv.at[which, 2 - hop, :, columns(head)],
            send_sem=fs_sem.at[hop - 1, which, head],
            recv_sem=fr_sem.at[hop - 1, which, head],
            device_id=place(lax.rem(me + hop, devices)),
            device_id_type=MESH,
        )

    def backward(hop, which, head):
        return pltpu.make_async_remote_copy(
            src_ref=term.at[which, 2 - hop, :, columns(head)],
            dst_ref=back.at[which, hop - 1, :, columns(head)],
            send_sem=bs_sem.at[hop - 1, which, head],
            recv_sem=br_sem.at[hop - 1, which, head],
            device_id=place(lax.rem(me - hop + devices, devices)),
            device_id_type=MESH,
        )

    near = (jnp.minimum(me, 1) + jnp.minimum(me // 2, 1)
            + jnp.minimum(devices - 1 - me, 1) + jnp.minimum((devices - 1 - me) // 2, 1))
    pl.semaphore_wait(barrier, near + (RING - 1) + (NEAR - 1) + 1 + (zgroup % 2))

    @pl.when(zgroup == 1)
    def _():
        for other in (0, 2):
            pl.semaphore_signal(ready, inc=1, device_id=place(group_peer(other)), device_id_type=MESH)

    def send_keys(head):
        for hop in (1, 2):
            @pl.when(me + hop < devices)
            def _():
                for which in (0, 1):
                    forward(hop, which, head).start()

    def send_terms(head):
        for hop in (1, 2):
            @pl.when(me >= hop)
            def _():
                for which in (0, 1):
                    backward(hop, which, head).start()

    @pl.loop(0, heads)
    def _(head):
        send_keys(head)

    for hop in (1, 2):
        @pl.when(me < hop)
        def _():
            kv[:, 2 - hop] = jnp.zeros((2, TOK, heads * HEAD), BF16)

        @pl.when(me + hop >= devices)
        def _():
            back[:, hop - 1] = jnp.zeros((2, TOK, heads * HEAD), BF16)

    wide = -(-docs // 128) * 128
    lens = jnp.concatenate([lens_ref[...], jnp.zeros((1, wide - docs), jnp.int32)], 1).astype(F32)
    down = lax.broadcasted_iota(jnp.int32, (wide, wide), 0)
    along = lax.broadcasted_iota(jnp.int32, (wide, wide), 1)
    real_down = lax.broadcasted_iota(jnp.int32, (wide, 1), 0) < docs
    real_along = lax.broadcasted_iota(jnp.int32, (1, wide), 1) < docs
    lens_all = jnp.broadcast_to(lens, (wide, wide))
    lens_col = jnp.sum(jnp.where(down == along, lens_all, 0.0), axis=1, keepdims=True)
    ends_row = jnp.sum(jnp.where(down <= along, lens_col, 0.0), axis=0, keepdims=True)
    ends_col = jnp.sum(jnp.where(along <= down, lens_all, 0.0), axis=1, keepdims=True)
    ends_row = jnp.where(real_along, ends_row, 1e9)
    ends_col = jnp.where(real_down, ends_col, 1e9)
    first = (me - 2) * TOK
    key_tok = (first + lax.broadcasted_iota(jnp.int32, (KEYS, 1), 0)).astype(F32)
    own_tok = (first + WINDOW + lax.broadcasted_iota(jnp.int32, (1, TOK), 1)).astype(F32)
    key_before = ends_row <= key_tok
    key_start = jnp.max(jnp.where(key_before, ends_row, 0.0), axis=1, keepdims=True)
    key_doc = jnp.sum(jnp.where(key_before, 1.0, 0.0), axis=1, keepdims=True)
    own_doc = jnp.sum(jnp.where(ends_col <= own_tok, 1.0, 0.0), axis=0, keepdims=True)
    apart = own_tok - key_tok
    visible = (key_doc == own_doc) & (apart >= 0.0) & (apart < float(WINDOW)) & (key_tok >= 0.0)
    bias[...] = jnp.where(visible, 0.0, MASKED)
    angle = (key_tok - key_start) * freq_ref[...]
    cosd[...] = jnp.cos(angle)
    front = lax.broadcasted_iota(jnp.int32, (1, HEAD), 1) < HALF
    sine = jnp.sin(angle)
    sins[...] = jnp.where(front, -sine, sine)

    for load in loads:
        load.wait()

    kgain = kgain_ref[...]
    qgain = qgain_ref[...]
    own = pl.ds(WINDOW, TOK)

    share = jnp.full((HEAD, HEAD), 1.0 / HEAD, BF16)

    def mean(values):
        high = values.astype(BF16)
        low = (values - high.astype(F32)).astype(BF16)
        return mm(high, share, NN) + mm(low, share, NN)

    def scale_of(values):
        return lax.rsqrt(mean(values * values) + EPS)

    def rotate(normed, cosine, sine):
        return normed * cosine + pltpu.roll(normed, HALF, 1) * sine

    def unrotate(grads, cosine, sine):
        return grads * cosine - pltpu.roll(grads, HALF, 1) * sine

    def raw_grad(grad_normed, unit, scale, gain):
        weighted = grad_normed * gain
        return scale * (weighted - unit * mean(weighted * unit))

    @pl.loop(0, heads)
    def _(head):
        cosine, sine = cosd[own, :], sins[own, :]
        raw = kv[0, 2, :, columns(head)].astype(F32)
        scale = scale_of(raw)
        k_scales[head] = scale
        k_rots[head] = rotate(raw * scale * kgain, cosine, sine).astype(BF16)
        for i in range(group):
            raw = q[:, columns(head * group + i)].astype(F32)
            scale = scale_of(raw)
            q_scales[head, pl.ds(i * TOK, TOK), :] = scale
            q_rots[head, pl.ds(i * TOK, TOK), :] = rotate(raw * scale * qgain, cosine, sine).astype(BF16)

    hold = HOLD

    def head_step(head, sums):
        q_sum, k_sum = sums
        for hop in (1, 2):
            @pl.when(me >= hop)
            def _():
                for which in (0, 1):
                    forward(hop, which, head).wait_recv()

        cols = columns(head)
        keys = kv[0, :2, :, cols].reshape(WINDOW, HEAD).astype(F32)
        values = kv[1, :, :, cols].reshape(KEYS, HEAD)
        k_unit = keys * scale_of(keys)
        past = pl.ds(0, WINDOW)
        k_rot = jnp.concatenate([rotate(k_unit * kgain, cosd[past, :], sins[past, :]).astype(BF16), k_rots[head]], 0)
        k_unit = jnp.concatenate([k_unit, kv[0, 2, :, cols].astype(F32) * k_scales[head]], 0)
        q_cols = [columns(head * group + i) for i in range(group)]
        q_rot = q_rots[head]
        g_out = jnp.concatenate([go[:, c] for c in q_cols], 0)
        masks = jnp.concatenate([bias[...]] * group, 1)
        scores = mm(k_rot, q_rot, NT) + masks
        prob_grad = mm(values, g_out, NT)
        top = jnp.max(scores, axis=0, keepdims=True)
        exps = jnp.exp2((scores - top) * (SCALE * LOG2E))
        probs = exps * (1.0 / jnp.sum(exps, axis=0, keepdims=True))
        delta = jnp.sum(probs * prob_grad, axis=0, keepdims=True)
        score_grad = (probs * (prob_grad - delta)).astype(BF16)
        v_term = mm(probs.astype(BF16), g_out, NN)
        k_term = mm(score_grad, q_rot, NN) * SCALE
        q_term = mm(score_grad, k_rot, TN) * SCALE
        v_far = v_term[:WINDOW].astype(BF16)
        k_far = k_term[:WINDOW].astype(BF16)
        term[0, :, :, cols] = k_far.reshape(2, TOK, HEAD)
        term[1, :, :, cols] = v_far.reshape(2, TOK, HEAD)
        dkv[0, :, cols] = k_term[WINDOW:]
        dkv[1, :, cols] = v_term[WINDOW:]
        k_all = jnp.concatenate([k_far.astype(F32), k_term[WINDOW:]], 0)
        k_sum = k_sum + jnp.sum(unrotate(k_all, cosd[...], sins[...]) * k_unit, axis=0, keepdims=True)
        for i, c in enumerate(q_cols):
            scale = q_scales[head, pl.ds(i * TOK, TOK), :]
            unit = q[:, c].astype(F32) * scale
            normed = unrotate(q_term[i * TOK:(i + 1) * TOK], cosd[own, :], sins[own, :])
            q_sum = q_sum + jnp.sum(normed * unit, axis=0, keepdims=True)
            dq_ref[:, c] = raw_grad(normed, unit, scale, qgain).astype(BF16)

        for hop in (1, 2):
            @pl.when((me >= hop) & (head >= hold))
            def _():
                for which in (0, 1):
                    backward(hop, which, head - hold).start()

        return q_sum, k_sum

    zero = jnp.zeros((1, HEAD), F32)
    q_sum, k_sum = lax.fori_loop(0, heads, head_step, (zero, zero))

    part = jnp.concatenate([q_sum, k_sum], 0)

    def message(source, target, index, peer, sem):
        return pltpu.make_async_remote_copy(
            src_ref=source, dst_ref=target, send_sem=as_sem.at[index], recv_sem=ar_sem.at[sem],
            device_id=place(peer), device_id_type=MESH,
        )

    def summed(values):
        out = values[0]
        for value in values[1:]:
            out = out + value
        return out

    pending = []

    def launch(part, base, count, mine, peer):
        box[base + mine] = part
        for i in range(1, count):
            copy = message(box.at[base + mine], box.at[base + mine], base + i, peer(i), base + mine)
            copy.start()
            pending.append(copy)

    def collect(base, count, mine, peer):
        for i in range(1, count):
            there = base + (mine + i) % count
            message(box.at[there], box.at[there], base + i, peer(i), there).wait_recv()
        return summed([box[base + i] for i in range(count)])

    dq_copy = pltpu.make_async_copy(dq_ref, dq_hbm, out_sem.at[0])
    launch(part, 0, RING, slot_in_ring, ring_peer)
    dq_copy.start()
    send_terms(heads - hold)
    send_terms(heads - hold + 1)
    part = collect(0, RING, slot_in_ring, ring_peer)
    launch(part, RING, NEAR, near_slot, near_peer)
    send_terms(heads - hold + 2)
    part = collect(RING, NEAR, near_slot, near_peer)
    last = RING + NEAR

    def far_peer(i):
        return group_peer((zgroup + i) % 3)

    @pl.when(zgroup != 1)
    def _():
        pl.semaphore_wait(ready, 1)

    launch(part, last, 3, zgroup, far_peer)

    @pl.loop(heads - hold + 3, heads)
    def _(head):
        send_terms(head)

    @pl.loop(0, heads)
    def _(head):
        for hop in (1, 2):
            @pl.when(me + hop < devices)
            def _():
                for which in (0, 1):
                    backward(hop, which, head).wait_recv()

        cols = columns(head)
        k_grad = dkv[0, :, cols] + back[0, 0, :, cols].astype(F32) + back[0, 1, :, cols].astype(F32)
        v_grad = dkv[1, :, cols] + back[1, 0, :, cols].astype(F32) + back[1, 1, :, cols].astype(F32)
        dv_ref[:, cols] = v_grad.astype(BF16)
        scale = k_scales[head]
        unit = kv[0, 2, :, cols].astype(F32) * scale
        normed = unrotate(k_grad, cosd[own, :], sins[own, :])
        dk_ref[:, cols] = raw_grad(normed, unit, scale, kgain).astype(BF16)

    outs = [pltpu.make_async_copy(dk_ref, dk_hbm, out_sem.at[1]), pltpu.make_async_copy(dv_ref, dv_hbm, out_sem.at[2])]
    for out in outs:
        out.start()
    gains_ref[...] = collect(last, 3, zgroup, far_peer)
    for copy in pending:
        copy.wait_send()
    dq_copy.wait()
    for out in outs:
        out.wait()

    for hop in (1, 2):
        @pl.when(me + hop < devices)
        def _():
            for head in range(heads):
                for which in (0, 1):
                    forward(hop, which, head).wait_send()

        @pl.when(me >= hop)
        def _():
            for head in range(heads):
                for which in (0, 1):
                    backward(hop, which, head).wait_send()


def finish(dq_in, dk_in, dv_in, gains_in, dq, dk, dv, q_gain, k_gain, sems):
    copies = [
        pltpu.make_async_copy(dq_in, dq, sems.at[0]),
        pltpu.make_async_copy(dk_in, dk, sems.at[1]),
        pltpu.make_async_copy(dv_in, dv, sems.at[2]),
    ]
    for copy in copies:
        copy.start()
    q_gain[...] = gains_in[0:1, :]
    k_gain[...] = gains_in[1:2, :]
    for copy in copies:
        copy.wait()


def on_device(devices, doc_lengths, query_raw, key_raw, value_matrix, out_grad, query_gain, key_gain):
    heads = key_raw.shape[1] // HEAD
    group = query_raw.shape[1] // key_raw.shape[1]
    docs = doc_lengths.shape[0]
    lens = doc_lengths.reshape(1, docs)
    lane = np.arange(HEAD) % HALF
    freq = jnp.asarray((np.float64(BASE) ** (-2.0 * lane / HEAD)).astype(np.float32).reshape(1, HEAD))
    vmem = pl.BlockSpec(memory_space=pltpu.VMEM)
    anywhere = pl.BlockSpec(memory_space=pl.ANY)
    width = heads * HEAD
    grad_query, grad_key, grad_value, gains = pl.pallas_call(
        functools.partial(kernel, devices, docs, heads, group),
        out_shape=(
            jax.ShapeDtypeStruct(query_raw.shape, BF16),
            jax.ShapeDtypeStruct(key_raw.shape, BF16),
            jax.ShapeDtypeStruct(key_raw.shape, BF16),
            jax.ShapeDtypeStruct((2, HEAD), F32),
        ),
        in_specs=[vmem] * 4 + [anywhere] * 4,
        out_specs=(anywhere, anywhere, anywhere, vmem),
        scratch_shapes=[
            pltpu.VMEM((TOK, width * group), BF16),
            pltpu.VMEM((TOK, width), BF16),
            pltpu.VMEM((TOK, width), BF16),
            pltpu.VMEM((TOK, width * group), BF16),
            pltpu.VMEM((TOK, width * group), BF16),
            pltpu.VMEM((2, 3, TOK, width), BF16),
            pltpu.VMEM((2, TOK, width), F32),
            pltpu.VMEM((2, 2, TOK, width), BF16),
            pltpu.VMEM((2, 2, TOK, width), BF16),
            pltpu.VMEM((KEYS, HEAD), F32),
            pltpu.VMEM((KEYS, HEAD), F32),
            pltpu.VMEM((KEYS, HEAD), F32),
            pltpu.VMEM((heads, group * TOK, HEAD), BF16),
            pltpu.VMEM((heads, group * TOK, HEAD), F32),
            pltpu.VMEM((heads, TOK, HEAD), BF16),
            pltpu.VMEM((heads, TOK, HEAD), F32),
            pltpu.VMEM((RING + NEAR + 3, 2, HEAD), F32),
            pltpu.SemaphoreType.DMA((4,)),
            pltpu.SemaphoreType.DMA((2, 2, heads)),
            pltpu.SemaphoreType.DMA((2, 2, heads)),
            pltpu.SemaphoreType.DMA((2, 2, heads)),
            pltpu.SemaphoreType.DMA((2, 2, heads)),
            pltpu.SemaphoreType.DMA((RING + NEAR + 3,)),
            pltpu.SemaphoreType.DMA((RING + NEAR + 3,)),
            pltpu.SemaphoreType.DMA((3,)),
            pltpu.SemaphoreType.REGULAR,
        ],
        compiler_params=pltpu.CompilerParams(
            collective_id=0, has_side_effects=True, vmem_limit_bytes=56 << 20
        ),
    )(lens, freq, query_gain.reshape(1, HEAD), key_gain.reshape(1, HEAD), query_raw, key_raw, value_matrix, out_grad)
    grad_query, grad_key, grad_value, q_gain, k_gain = pl.pallas_call(
        finish,
        out_shape=(
            jax.ShapeDtypeStruct(query_raw.shape, BF16),
            jax.ShapeDtypeStruct(key_raw.shape, BF16),
            jax.ShapeDtypeStruct(key_raw.shape, BF16),
            jax.ShapeDtypeStruct((1, HEAD), F32),
            jax.ShapeDtypeStruct((1, HEAD), F32),
        ),
        in_specs=[vmem] * 4,
        out_specs=(anywhere, anywhere, anywhere, vmem, vmem),
        scratch_shapes=[pltpu.SemaphoreType.DMA((3,))],
    )(grad_query, grad_key, grad_value, gains)
    return grad_query, grad_key, grad_value, q_gain.reshape(HEAD), k_gain.reshape(HEAD)


def solution(mesh):
    devices = mesh.devices.size
    rows = P(("ctx", "grp"), None)
    return jax.shard_map(
        functools.partial(on_device, devices),
        mesh=mesh,
        in_specs=(P(), rows, rows, rows, rows, P(), P()),
        out_specs=(rows, rows, rows, P(), P()),
        check_vma=False,
    )
```
